32 devices in a mesh: dp: 8 (over z, y), mp: 4 (over x, core).
Axes of the slice: x: 2, y: 2, z: 4, core: 2. Of those that a mesh axis runs over, the one named last changes fastest.
Arguments:
- tokens: bfloat16 [128, 6656], P('dp', 'mp'), may hold values from -6 to 6
- grad_out: bfloat16 [128, 6656], P('dp', 'mp'), may hold values from -1.5 to 1.5
- gate_src: bfloat16 [10240, 6656], P(('dp', 'mp')), may hold values from -0.078125 to 0.078125
- up_src: bfloat16 [10240, 6656], P(('dp', 'mp')), may hold values from -0.078125 to 0.078125
- down_src: bfloat16 [10240, 6656], P(('dp', 'mp')), may hold values from -0.109375 to 0.109375
- unit_map: int32 [15360], P(('dp', 'mp')), may hold values from 0 to 10239, as said below
- copy_flag: int32 [15360], P(('dp', 'mp')), may hold values from 0 to 1, as said below
Outputs:
- layer_out: bfloat16 [128, 6656], P('dp', 'mp')
- grad_tokens: bfloat16 [128, 6656], P('dp', 'mp')
- grad_gate: bfloat16 [15360, 6656], P(('dp', 'mp'))
- grad_up: bfloat16 [15360, 6656], P(('dp', 'mp'))
- grad_down: bfloat16 [15360, 6656], P(('dp', 'mp'))
The draws below stay inside these ranges and needn't reach their ends.
Inputs may be any that keep to these rules, and one draw needn't show every extreme that they name: `unit_map`: the widened unit j lies on the device of flat index j // 480 along dp+mp, and its source unit lies on a device with the same mp index. Every source unit is the source of one or two widened units. For every pair of devices, at most 60 widened units of the one have their source on the other; every device takes exactly 60 from some device and gives exactly 60 to some device. `copy_flag`: A source unit with one widened unit gives it flag 1; of a source's two widened units at least one has flag 1.
All inputs are finite; a program needn't handle non-finite values.
Results may differ from the reference program's by a relative error of at most 0.0049.
Values may be sent and summed in bfloat16 or wider, within the bound.
No kernel may reach another device: no remote copies, remote signals or barrier semaphores. Data moves between devices by JAX's collectives and lax.ppermute only.
A program may use at most 128 MiB of HBM per device.

```python
import jax
import jax.numpy as jnp
from jax import lax

D = 6656
FS = 10240
TOKENS = 128
FW = 15360
FS_DEV = 320
FW_DEV = 480
QUANT = 20
N_DP = 8
N_MP = 4


def mapping_tables(key):
    unit_map = jnp.zeros((FW,), jnp.int32)
    copy_flag = jnp.zeros((FW,), jnp.int32)
    members = FW_DEV // QUANT
    for group in range(N_MP):
        group_key = jax.random.fold_in(key, 7000 + group)
        scores = jax.random.permutation(jax.random.fold_in(group_key, 1), 3 * N_DP).astype(jnp.int32)
        cell = jnp.arange(3 * N_DP, dtype=jnp.int32)
        offset = cell % N_DP
        layer = cell // N_DP
        first = scores[0] % N_DP
        scores = jnp.where(offset == first, layer - 3, scores)
        scores = jnp.where((offset == 1) & (layer == 0), -10, scores)
        scores = jnp.where((offset == N_DP // 2) & (layer == 0), -9, scores)
        scores = jnp.where((offset == N_DP - 1) & (layer == 0), -8, scores)
        order = jnp.argsort(scores)
        chosen = jnp.zeros((3 * N_DP,), jnp.int32).at[order[:members]].set(1)
        multiple = chosen.reshape(3, N_DP).sum(0)
        devices = jnp.arange(N_DP, dtype=jnp.int32)
        counts = QUANT * multiple[(devices[None, :] - devices[:, None]) % N_DP]
        before = jnp.cumsum(counts, axis=1) - counts

        def owner_lists(owner):
            owner_key = jax.random.fold_in(group_key, 100 + owner)
            extra = jax.random.permutation(jax.random.fold_in(owner_key, 1), FS_DEV)[:FS_DEV // 2].astype(jnp.int32)
            local = jnp.concatenate([jnp.arange(FS_DEV, dtype=jnp.int32), extra])
            coins = jax.random.randint(jax.random.fold_in(owner_key, 2), (FS_DEV // 2,), 0, 2).astype(jnp.int32)
            flags = jnp.concatenate([jnp.ones((FS_DEV,), jnp.int32), coins])
            shuffle = jax.random.permutation(jax.random.fold_in(owner_key, 3), FW_DEV)
            return (local[shuffle], flags[shuffle])
        owner_local, owner_flags = jax.vmap(owner_lists)(devices)

        def dest_shuffle(dest):
            return jax.random.permutation(jax.random.fold_in(group_key, 5000 + dest), FW_DEV).astype(jnp.int32)
        shuffles = jax.vmap(dest_shuffle)(devices)
        column = counts.T
        ends = jnp.cumsum(column, axis=1)
        starts = ends - column
        slot = jnp.arange(FW_DEV, dtype=jnp.int32)
        target = jnp.sum((slot[None, :, None] >= ends[:, None, :]).astype(jnp.int32), axis=2)
        position = slot[None, :] - jnp.take_along_axis(starts, target, axis=1)
        place = jnp.take_along_axis(before.T, target, axis=1) + position
        unit_local = shuffles[target, place]
        widened = (target * N_MP + group) * FW_DEV + unit_local
        source = (devices[:, None] * N_MP + group) * FS_DEV + owner_local
        unit_map = unit_map.at[widened.reshape(-1)].set(source.reshape(-1))
        copy_flag = copy_flag.at[widened.reshape(-1)].set(owner_flags.reshape(-1))
    return (unit_map, copy_flag)


def draw_unit_map(key, part):
    return mapping_tables(jax.random.fold_in(key, 11))[0]


def draw_copy_flag(key, part):
    return mapping_tables(jax.random.fold_in(key, 11))[1]


def draw_tokens(key, part):
    noise = jax.random.normal(jax.random.fold_in(key, 21), (TOKENS, D), jnp.float32)
    values = noise
    return jnp.clip(values, -6.0, 6.0).astype(jnp.bfloat16)


def draw_grad_out(key, part):
    noise = jax.random.normal(jax.random.fold_in(key, 31), (TOKENS, D), jnp.float32)
    values = 0.25 * noise
    return jnp.clip(values, -1.5, 1.5).astype(jnp.bfloat16)


def raised(values, key, source, target, parts, factor):
    owner, partner = [(jnp.arange(values.shape[dim]) // (values.shape[dim] // parts)).reshape([-1 if axis == dim else 1 for axis in range(values.ndim)]) for dim in (source, target)]
    chosen = jax.random.permutation(key, parts)[partner]
    strong = (owner == chosen) | (owner == (partner + parts // 2) % parts)
    return jnp.where(strong, factor * values, values)


def block_scale(stream_key, shape, shards, least, top_value):
    loudness, own = 1.0, jax.random.fold_in(stream_key, 6)
    for dim, parts in shards:
        draws = jnp.exp(jax.random.uniform(jax.random.fold_in(own, dim), (parts,), jnp.float32, least / len(shards), top_value / len(shards)))
        loudness = loudness * jnp.repeat(draws, shape[dim] // parts).reshape([-1 if axis == dim else 1 for axis in range(len(shape))])
    return loudness


def scatter_about(key, extent, width, limit, split=(), kind=jnp.bfloat16):
    factor_of = block_scale(key, extent, split, -0.22, 0.18) if split else 1.0
    drawn = jax.random.normal(key, extent, jnp.float32) * width * factor_of
    return jnp.minimum(jnp.maximum(drawn, -limit), limit).astype(kind)


def heavy_noise(own_key, shape, scale, bound, cuts, heavy, held_as=jnp.bfloat16):
    array = scale * jax.random.normal(own_key, shape, jnp.float32)
    if cuts:
        array = array * block_scale(own_key, shape, cuts, -0.22, 0.18)
    return jnp.clip(raised(array, jax.random.fold_in(own_key, 3), *heavy), -bound, bound).astype(held_as)


def setup_inputs(seed: int = 0) -> dict:
    splits = jax.random.split(jax.random.key(seed), 8)
    tokens = draw_tokens(jax.random.fold_in(splits[7], 71), 0)
    grad_out = draw_grad_out(jax.random.fold_in(splits[7], 71), 0)
    gate_src = scatter_about(splits[2], (FS, D), D ** -0.5, 0.078125, ((0, 32),))
    up_src = scatter_about(splits[3], (FS, D), D ** -0.5, 0.078125, ((0, 32),))
    down_src = heavy_noise(splits[4], (FS, D), FS ** -0.5, 0.109375, ((0, 32),), (0, 1, 32, 2.75))
    unit_map = draw_unit_map(jax.random.fold_in(splits[7], 71), 0)
    copy_flag = draw_copy_flag(jax.random.fold_in(splits[7], 71), 0)
    return {"tokens": tokens, "grad_out": grad_out, "gate_src": gate_src, "up_src": up_src, "down_src": down_src, "unit_map": unit_map, "copy_flag": copy_flag}


def reference(tokens, grad_out, gate_src, up_src, down_src, unit_map, copy_flag):
    flags = copy_flag.astype(jnp.float32)
    share = jax.ops.segment_sum(flags, unit_map, num_segments=FS)
    scale = flags / share[unit_map]
    dims = (((1,), (1,)), ((), ()))
    pre_gate = lax.dot_general(tokens, gate_src, dims, preferred_element_type=jnp.float32)
    pre_up = lax.dot_general(tokens, up_src, dims, preferred_element_type=jnp.float32)
    sigma = jax.nn.sigmoid(pre_gate)
    active = pre_gate * sigma
    hidden = (active * pre_up).astype(jnp.bfloat16)
    layer_out = jnp.dot(hidden, down_src, preferred_element_type=jnp.float32).astype(jnp.bfloat16)
    grad_hidden = lax.dot_general(grad_out, down_src, dims, preferred_element_type=jnp.float32)
    grad_pre_gate = (grad_hidden * pre_up * (sigma + active * (1.0 - sigma))).astype(jnp.bfloat16)
    grad_pre_up = (grad_hidden * active).astype(jnp.bfloat16)
    grad_tokens = jnp.dot(grad_pre_gate, gate_src, preferred_element_type=jnp.float32)
    grad_tokens = grad_tokens + jnp.dot(grad_pre_up, up_src, preferred_element_type=jnp.float32)
    tdims = (((0,), (0,)), ((), ()))
    gate_rows = lax.dot_general(grad_pre_gate, tokens, tdims, preferred_element_type=jnp.float32).astype(jnp.bfloat16)
    up_rows = lax.dot_general(grad_pre_up, tokens, tdims, preferred_element_type=jnp.float32).astype(jnp.bfloat16)
    down_rows = lax.dot_general(hidden, grad_out, tdims, preferred_element_type=jnp.float32).astype(jnp.bfloat16)
    scale_bf = scale.astype(jnp.bfloat16)[:, None]
    grad_gate = gate_rows[unit_map] * scale_bf
    grad_up = up_rows[unit_map] * scale_bf
    grad_down = down_rows[unit_map]
    return layer_out, grad_tokens.astype(jnp.bfloat16), grad_gate, grad_up, grad_down
```

```python
import functools

import jax
import jax.numpy as jnp
from jax import lax
from jax.experimental import pallas as pl
from jax.experimental.pallas import tpu as pltpu
from jax.sharding import PartitionSpec as P


F32 = jnp.float32
BF16 = jnp.bfloat16
LIMIT = 60 * 1024 * 1024
NT = (((1,), (1,)), ((), ()))
NN = (((1,), (0,)), ((), ()))


def dot(a, b, dims=NN):
    return lax.dot_general(a, b, dims, preferred_element_type=F32)


def swap(x, axis, offset):
    n = lax.axis_size(axis)
    return lax.ppermute(x, axis, [(i, i ^ offset) for i in range(n)])


def outer_stages(n):
    stages, stride = [], 2
    while stride < n:
        radix = 4 if stride * 4 <= n else 2
        stages.append((stride, radix))
        stride *= radix
    return stages


def token_order(dp, n_dp, rows):
    half = n_dp // 2
    tokens = n_dp * rows
    place = lax.broadcasted_iota(jnp.int32, (tokens, tokens), 0)
    held = lax.broadcasted_iota(jnp.int32, (tokens, tokens), 1)
    block = held // rows
    offset = block // half + 2 * (block % half)
    return (place == (dp ^ offset) * rows + held % rows).astype(F32).astype(BF16)


def cols_of(index, width):
    return pl.ds(pl.multiple_of(index * width, 128), width)


def cot_block(cots, m):
    lo, hi = m % 2, m // 2
    return jnp.concatenate([cots[2 * lo][hi], cots[2 * lo + 1][hi]], axis=0)


def forward_kernel(n_dp, n_mp, rows, *refs):
    toks, refs = refs[:n_mp], refs[n_mp:]
    cots, refs = refs[:4], refs[4:]
    gate, up, down, pick, hid_o, gpg_o, gpu_o, send_o = refs
    mp = lax.axis_index("mp")
    dp = lax.axis_index("dp")
    width = toks[0].shape[1]
    pre_gate = pre_up = grad_hidden = 0.0
    for m in range(n_mp):
        cols = cols_of(mp ^ m, width)
        t = toks[m][...]
        pre_gate = pre_gate + dot(t, gate[:, cols], NT)
        pre_up = pre_up + dot(t, up[:, cols], NT)
        grad_hidden = grad_hidden + dot(cot_block(cots, m), down[:, cols], NT)
    sigma = jax.nn.sigmoid(pre_gate)
    active = pre_gate * sigma
    hid = (active * pre_up).astype(BF16)
    gpg = (grad_hidden * pre_up * (sigma + active * (1.0 - sigma))).astype(BF16)
    gpu = (grad_hidden * active).astype(BF16)
    hid_o[...] = hid
    gpg_o[...] = gpg
    gpu_o[...] = gpu
    order = token_order(dp, n_dp, rows)
    chosen = pick[...] == lax.broadcasted_iota(
        jnp.int32, (pick.shape[0], hid.shape[1]), 1
    )
    chosen = chosen.astype(F32).astype(BF16)
    for i, act in enumerate((gpg, gpu, hid)):
        placed = dot(order, act).astype(BF16)
        tokens = placed.shape[0]
        send_o[:, i * tokens : (i + 1) * tokens] = dot(chosen, placed, NT).astype(BF16)


def partial_kernel(n_mp, n_terms, *refs):
    acts, refs = refs[:n_terms], refs[n_terms:]
    weights, refs = refs[:n_terms], refs[n_terms:]
    keep, send = refs
    mp = lax.axis_index("mp")
    width = keep.shape[2]
    for m in range(n_mp):
        cols = cols_of(mp ^ m, width)
        total = dot(acts[0][...], weights[0][:, cols])
        for a, w in zip(acts[1:], weights[1:]):
            total = total + dot(a[...], w[:, cols])
        if m % 2:
            send[m // 2] = total.astype(BF16)
        else:
            keep[m // 2] = total


def widen_kernel(n_dp, n_mp, rows, *refs):
    toks, refs = refs[:n_mp], refs[n_mp:]
    cots, refs = refs[:4], refs[4:]
    moved, row, scale, gate_o, up_o, down_o, buf, sem = refs
    mp = lax.axis_index("mp")
    dp = lax.axis_index("dp")
    tokens, width = toks[0].shape
    order = token_order(dp, n_dp, rows)
    chosen = row[...] == lax.broadcasted_iota(
        jnp.int32, (row.shape[0], moved.shape[0]), 1
    )
    chosen = chosen.astype(F32).astype(BF16)
    acts = []
    for i in range(3):
        act = dot(chosen, moved[:, i * tokens : (i + 1) * tokens])
        if i < 2:
            act = act * scale[...]
        acts.append(dot(act.astype(BF16), order).astype(BF16))
    outs = (gate_o, up_o, down_o)
    slots = buf.shape[0]
    copies = []
    step = 0
    for m in range(n_mp):
        cols = cols_of(mp ^ m, width)
        for i in range(3):
            slot = step % slots
            if step >= slots:
                copies[step - slots].wait()
            right = toks[m] if i < 2 else None
            for c in range(0, width, 256):
                e = min(c + 256, width)
                if i < 2:
                    block = toks[m][:, c:e]
                else:
                    lo, hi = m % 2, m // 2
                    block = jnp.concatenate(
                        [cots[2 * lo][hi, :, c:e], cots[2 * lo + 1][hi, :, c:e]], axis=0
                    )
                buf[slot, :, c:e] = dot(acts[i], block).astype(BF16)
            copy = pltpu.make_async_copy(
                buf.at[slot], outs[i].at[:, cols], sem.at[slot]
            )
            copy.start()
            copies.append(copy)
            step += 1
    for copy in copies[-slots:]:
        copy.wait()


VM = pl.BlockSpec(memory_space=pltpu.VMEM)
ANY = pl.BlockSpec(memory_space=pl.ANY)


def call(kernel, n_in, outs, out_specs, flops, nbytes, scratch=()):
    return pl.pallas_call(
        kernel,
        out_shape=outs,
        in_specs=[VM] * n_in,
        out_specs=out_specs,
        scratch_shapes=scratch,
        compiler_params=pltpu.CompilerParams(vmem_limit_bytes=LIMIT),
        cost_estimate=pl.CostEstimate(
            flops=flops, bytes_accessed=nbytes, transcendentals=0
        ),
    )


def per_device(tokens, grad_out, gate_src, up_src, down_src, unit_map, copy_flag):
    n_dp = lax.axis_size("dp")
    n_mp = lax.axis_size("mp")
    dp = lax.axis_index("dp")
    mp = lax.axis_index("mp")
    rows, width = tokens.shape
    src_dev = gate_src.shape[0]
    wide_dev = unit_map.shape[0]
    quant = (wide_dev + 3 * n_dp - 1) // (3 * n_dp)
    slots = 3 * quant
    my_flat = dp * n_mp + mp
    n_tok = rows * n_dp
    half = n_dp // 2
    stages = outer_stages(n_dp)

    digits, top = 1, 256
    while top < 2 * src_dev * n_dp * n_mp:
        digits, top = digits + 1, top * 256
    code = unit_map * 2 + copy_flag
    parts = jnp.concatenate([(code // 256**k) % 256 for k in range(digits)])
    lanes = -(-(digits * wide_dev) // (rows * 128)) * 128
    parts = jnp.pad(parts, (0, rows * lanes - digits * wide_dev))
    parts = parts.astype(F32).astype(BF16).reshape(rows, lanes)

    load = jnp.concatenate([tokens, parts, grad_out], axis=1)
    for stride, radix in stages:
        load = jnp.concatenate(
            [load] + [swap(load, "dp", r * stride) for r in range(1, radix)], axis=0
        )
    t_own = load[:, : width + lanes]
    c_own = load[:, width + lanes :]
    t_far = swap(t_own, "dp", 1)
    c_hi = jnp.stack([c_own] + [swap(c_own, "mp", 2 * r) for r in range(1, n_mp // 2)])
    t_all = jnp.concatenate([t_own[:, :width], t_far[:, :width]], axis=0)
    t_hi = [t_all] + [swap(t_all, "mp", 2 * r) for r in range(1, n_mp // 2)]
    c_far = swap(c_hi, "dp", 1)
    toks = []
    for t in t_hi:
        toks += [t, swap(t, "mp", 1)]
    cots = [c_hi, c_far, swap(c_hi, "mp", 1), swap(c_far, "mp", 1)]

    held = jnp.stack([t_own[:, width:], t_far[:, width:]]).astype(F32).astype(jnp.int32)
    held = held.reshape(2, half, rows * lanes)[:, :, : digits * wide_dev]
    held = held.reshape(2, half, digits, wide_dev)
    codes = sum(held[:, :, k] * 256**k for k in range(digits))
    codes = codes.transpose(1, 0, 2).reshape(n_dp, wide_dev)
    codes = lax.optimization_barrier(codes)
    maps = codes // 2
    flags = codes % 2
    share = jnp.sum(
        jnp.where(
            (maps.reshape(-1)[None, :] == unit_map[:, None]), flags.reshape(-1)[None, :], 0
        ),
        axis=1,
    )
    scale = copy_flag.astype(F32) / share.astype(F32)
    owner_dp = unit_map // src_dev // n_mp
    unit_index = jnp.arange(wide_dev, dtype=jnp.int32)
    earlier = (owner_dp[:, None] == owner_dp[None, :]) & (
        unit_index[:, None] > unit_index[None, :]
    )
    recv_row = owner_dp * slots + jnp.sum(earlier.astype(jnp.int32), axis=1)
    requests = jnp.take(maps, jnp.arange(n_dp, dtype=jnp.int32) ^ dp, axis=0)
    owned = requests // src_dev == my_flat
    rank = jnp.cumsum(owned.astype(jnp.int32), axis=1) - 1
    slot_ids = jnp.arange(slots, dtype=jnp.int32)
    placed = owned[:, None, :] & (rank[:, None, :] == slot_ids[None, :, None])
    local = requests - my_flat * src_dev
    pick = jnp.sum(jnp.where(placed, local[:, None, :], 0), axis=2).reshape(-1, 1)

    act = jax.ShapeDtypeStruct((n_tok, src_dev), BF16)
    load_rows = n_dp * slots
    wbytes = src_dev * width * n_mp * 2
    mm = 2 * n_tok * src_dev * width * n_mp
    hid, gpg, gpu, send = call(
        functools.partial(forward_kernel, n_dp, n_mp, rows),
        n_mp + 8,
        (act, act, act, jax.ShapeDtypeStruct((load_rows, 3 * n_tok), BF16)),
        (VM,) * 4,
        3 * mm,
        3 * wbytes,
    )(*toks, *cots, gate_src, up_src, down_src, pick)
    moved = lax.all_to_all(send, "dp", split_axis=0, concat_axis=0, tiled=True)

    keep_t = jax.ShapeDtypeStruct((n_mp // 2, n_tok, width), F32)
    send_t = jax.ShapeDtypeStruct((n_mp // 2, n_tok, width), BF16)

    def partial(acts, weights):
        k = len(acts)
        return call(
            functools.partial(partial_kernel, n_mp, k),
            2 * k,
            (keep_t, send_t),
            (VM, VM),
            k * mm,
            k * wbytes,
        )(*acts, *weights)

    out_keep, out_send = partial((hid,), (down_src,))
    in_keep, in_send = partial((gpg, gpu), (gate_src, up_src))

    def scatter(total, axis, stride, radix):
        parts = total.reshape((radix, -1) + total.shape[1:])
        out = parts[0]
        got = [
            swap(parts[r].astype(BF16), axis, r * stride) for r in range(1, radix)
        ]
        for g in got:
            out = out + g.astype(F32)
        return out

    out_sum = out_keep + swap(out_send, "mp", 1).astype(F32)
    in_sum = in_keep + swap(in_send, "mp", 1).astype(F32)
    out_sum = scatter(out_sum, "mp", 2, n_mp // 2)[0]
    out_sum = scatter(out_sum, "dp", 1, 2)
    in_rows = in_sum.transpose(1, 0, 2)
    in_rows = scatter(in_rows, "dp", 1, 2)
    in_sum = scatter(in_rows.transpose(1, 0, 2), "mp", 2, n_mp // 2)[0]
    both = jnp.concatenate([out_sum, in_sum], axis=1)
    for stride, radix in reversed(stages):
        both = scatter(both, "dp", stride, radix)

    wide_t = jax.ShapeDtypeStruct((wide_dev, n_mp * width), BF16)
    grad_gate, grad_up, grad_down = call(
        functools.partial(widen_kernel, n_dp, n_mp, rows),
        n_mp + 7,
        (wide_t,) * 3,
        (ANY,) * 3,
        6 * n_tok * wide_dev * width * n_mp,
        3 * wide_dev * width * n_mp * 2,
        (pltpu.VMEM((6, wide_dev, width), BF16), pltpu.SemaphoreType.DMA((6,))),
    )(*toks, *cots, moved, recv_row.reshape(-1, 1), scale.reshape(-1, 1))
    return (
        both[:, :width].astype(BF16),
        both[:, width:].astype(BF16),
        grad_gate,
        grad_up,
        grad_down,
    )


def solution(mesh):
    rows = P(("dp", "mp"), None)
    tile = P("dp", "mp")
    unit = P(("dp", "mp"))
    return jax.shard_map(
        per_device,
        mesh=mesh,
        in_specs=(tile, tile, rows, rows, rows, unit, unit),
        out_specs=(tile, tile, rows, rows, rows),
        check_vma=False,
    )
```

```python
import functools

import jax
import jax.numpy as jnp
from jax import lax
from jax.experimental import pallas as pl
from jax.experimental.pallas import tpu as pltpu
from jax.sharding import PartitionSpec as P


F32 = jnp.float32
BF16 = jnp.bfloat16
LIMIT = 12 * 1024 * 1024
NT = (((1,), (1,)), ((), ()))
NN = (((1,), (0,)), ((), ()))


def dot(a, b, dims=NN):
    return lax.dot_general(a, b, dims, preferred_element_type=F32)


def swap(x, axis, offset):
    n = lax.axis_size(axis)
    return lax.ppermute(x, axis, [(i, i ^ offset) for i in range(n)])


def outer_stages(n):
    stages, stride = [], 2
    while stride < n:
        radix = 4 if stride * 4 <= n else 2
        stages.append((stride, radix))
        stride *= radix
    return stages


def token_order(dp, n_dp, rows):
    half = n_dp // 2
    tokens = n_dp * rows
    place = lax.broadcasted_iota(jnp.int32, (tokens, tokens), 0)
    held = lax.broadcasted_iota(jnp.int32, (tokens, tokens), 1)
    block = held // rows
    offset = block // half + 2 * (block % half)
    return (place == (dp ^ offset) * rows + held % rows).astype(F32).astype(BF16)


def cols_of(index, width):
    return pl.ds(pl.multiple_of(index * width, 128), width)


def pack_kernel(digits, tok, cot, umap_i, flag_i, out, umap, flag, t_buf, c_buf, sem):
    rows, width = tok.shape
    wide = umap.shape[1]
    lanes = out.shape[1] - 2 * width
    moves = ((umap_i, umap), (flag_i, flag), (tok, t_buf), (cot, c_buf))
    copies = []
    for i, (src, dst) in enumerate(moves):
        copies.append(pltpu.make_async_copy(src, dst, sem.at[i]))
        copies[-1].start()
    copies[0].wait()
    copies[1].wait()
    code = umap[...] * 2 + flag[...]
    chunks = -(-wide // 128)
    code = jnp.concatenate(
        [code, jnp.zeros((1, chunks * 128 - wide), jnp.int32)], axis=1
    ) if chunks * 128 > wide else code
    parts = []
    for d in range(digits):
        digit = ((code >> (8 * d)) & 255).astype(F32)
        parts += [digit[:, 128 * c : 128 * c + 128] for c in range(chunks)]
    zero = jnp.zeros((1, 128), F32)
    parts += [zero] * (rows * lanes // 128 - len(parts))
    for b in range(lanes // 128):
        block = jnp.concatenate(parts[b * rows : (b + 1) * rows], axis=0)
        out[:, width + 128 * b : width + 128 * b + 128] = block.astype(BF16)
    copies[2].wait()
    out[:, :width] = t_buf[...]
    copies[3].wait()
    out[:, width + lanes :] = c_buf[...]


def table_kernel(digits, n_mp, rows, wide, src_dev, slots, near, far, pick_o, row_o, scale_o):
    mp = lax.axis_index("mp")
    dp = lax.axis_index("dp")
    half = near.shape[0] // rows
    chunks = -(-wide // 128)
    span = chunks * 128
    held = (near[...].astype(F32), far[...].astype(F32))

    def code_of(offset):
        part = held[offset % 2]
        first = (offset // 2) * rows
        pieces = []
        for c in range(chunks):
            total = 0.0
            for d in range(digits):
                k = d * chunks + c
                r, b = first + k % rows, k // rows
                total = total + part[r : r + 1, 128 * b : 128 * b + 128] * float(256**d)
            pieces.append(total)
        return jnp.concatenate(pieces, axis=1)

    n_dp = 2 * half
    code = jnp.concatenate([code_of(o) for o in range(n_dp)], axis=0).astype(jnp.int32)
    flags = (code & 1).astype(F32)
    maps = (code >> 1).astype(F32)
    lane = lax.broadcasted_iota(jnp.int32, (1, span), 1)
    valid = lane < wide
    lane_w = lax.broadcasted_iota(jnp.int32, (wide, span), 1)
    unit_w = lax.broadcasted_iota(jnp.int32, (wide, span), 0)
    eye = lane_w == unit_w

    def column(row):
        return jnp.sum(jnp.where(eye, row, 0.0), axis=1, keepdims=True)

    map_col = column(maps[0:1])
    flag_col = column(flags[0:1])
    share = jnp.zeros((wide, span), F32)
    for o in range(n_dp):
        share = share + jnp.where(maps[o : o + 1] == map_col, flags[o : o + 1], 0.0)
    share = jnp.sum(share, axis=1, keepdims=True)
    scale_o[...] = flag_col / share

    def owner_of(m):
        return jnp.floor((m + 0.5) * (1.0 / (src_dev * n_mp)))

    owner = jnp.where(valid, owner_of(maps[0:1]), -1.0)
    owner_col = owner_of(map_col)
    earlier = (owner == owner_col) & (lane_w < unit_w)
    arrival = jnp.sum(jnp.where(earlier, 1.0, 0.0), axis=1, keepdims=True)
    offset = owner_col.astype(jnp.int32) ^ dp
    place = (offset & 1) * half + (offset >> 1)
    row_o[...] = place * slots + arrival.astype(jnp.int32)

    local = maps - ((dp * n_mp + mp) * src_dev).astype(F32)
    owned = (local >= 0.0) & (local < float(src_dev)) & valid
    mine = jnp.where(owned, 1.0, 0.0)
    low = lax.broadcasted_iota(jnp.int32, (span, span), 0)
    high = lax.broadcasted_iota(jnp.int32, (span, span), 1)
    before = jnp.where(low < high, 1.0, 0.0).astype(BF16)
    rank = dot(mine.astype(BF16), before)
    rank = jnp.where(owned, rank, -1.0).astype(jnp.int32)
    slot = lax.broadcasted_iota(jnp.int32, (slots, span), 0)
    for o in range(n_dp):
        hit = jnp.where(rank[o : o + 1] == slot, local[o : o + 1] + 1.0, 0.0)
        chosen = jnp.sum(hit, axis=1, keepdims=True) - 1.0
        pick_o[o * slots : (o + 1) * slots, :] = chosen.astype(jnp.int32)


def near_kernel(n_mp, *refs):
    toks, refs = refs[:2], refs[2:]
    cots, refs = refs[:2], refs[2:]
    gate, up, down, gate_o, up_o, hid_o = refs
    mp = lax.axis_index("mp")
    width = toks[0].shape[1]
    pre_gate = pre_up = 0.0
    for m in range(2):
        cols = cols_of(mp ^ m, width)
        t = toks[m][...]
        pre_gate = pre_gate + dot(t, gate[:, cols], NT)
        pre_up = pre_up + dot(t, up[:, cols], NT)
    gate_o[...] = pre_gate
    up_o[...] = pre_up
    grad_hidden = 0.0
    for m in range(n_mp):
        cols = cols_of(mp ^ m, width)
        grad_hidden = grad_hidden + dot(cots[m % 2][m // 2], down[:, cols], NT)
    hid_o[...] = grad_hidden


def forward_kernel(n_dp, n_mp, rows, *refs):
    toks, refs = refs[: n_mp - 2], refs[n_mp - 2 :]
    cots, refs = refs[:2], refs[2:]
    gate_i, up_i, hid_i, gate, up, down, pick, hid_o, gpg_o, gpu_o, send_o = refs
    mp = lax.axis_index("mp")
    dp = lax.axis_index("dp")
    width = toks[0].shape[1]
    pre_gate, pre_up = gate_i[...], up_i[...]
    for m in range(2, n_mp):
        cols = cols_of(mp ^ m, width)
        t = toks[m - 2][...]
        pre_gate = pre_gate + dot(t, gate[:, cols], NT)
        pre_up = pre_up + dot(t, up[:, cols], NT)
    grad_hidden = 0.0
    for m in range(n_mp):
        cols = cols_of(mp ^ m, width)
        grad_hidden = grad_hidden + dot(cots[m % 2][m // 2], down[:, cols], NT)
    grad_hidden = jnp.concatenate([hid_i[...], grad_hidden], axis=0)
    sigma = jax.nn.sigmoid(pre_gate)
    active = pre_gate * sigma
    hid = (active * pre_up).astype(BF16)
    gpg = (grad_hidden * pre_up * (sigma + active * (1.0 - sigma))).astype(BF16)
    gpu = (grad_hidden * active).astype(BF16)
    hid_o[...] = hid
    gpg_o[...] = gpg
    gpu_o[...] = gpu
    order = token_order(dp, n_dp, rows)
    chosen = pick[...] == lax.broadcasted_iota(
        jnp.int32, (pick.shape[0], hid.shape[1]), 1
    )
    chosen = chosen.astype(F32).astype(BF16)
    for i, act in enumerate((gpg, gpu, hid)):
        placed = dot(order, act).astype(BF16)
        tokens = placed.shape[0]
        send_o[:, i * tokens : (i + 1) * tokens] = dot(chosen, placed, NT).astype(BF16)


def partial_kernel(n_mp, n_terms, *refs):
    acts, refs = refs[:n_terms], refs[n_terms:]
    weights, refs = refs[:n_terms], refs[n_terms:]
    keep, send = refs
    mp = lax.axis_index("mp")
    width = keep.shape[2]
    for m in range(n_mp):
        cols = cols_of(mp ^ m, width)
        total = dot(acts[0][...], weights[0][:, cols])
        for a, w in zip(acts[1:], weights[1:]):
            total = total + dot(a[...], w[:, cols])
        if m % 2:
            send[m // 2] = total.astype(BF16)
        else:
            keep[m // 2] = total


def widen_kernel(n_dp, n_mp, rows, n_moved, *refs):
    toks, refs = refs[:n_mp], refs[n_mp:]
    cots, refs = refs[:4], refs[4:]
    moved, refs = refs[:n_moved], refs[n_moved:]
    row, scale, gate_o, up_o, down_o, buf, sem = refs
    mp = lax.axis_index("mp")
    dp = lax.axis_index("dp")
    tokens, width = toks[0].shape
    order = token_order(dp, n_dp, rows)
    size = moved[0].shape[0]
    chosen = []
    for k in range(n_moved):
        ids = lax.broadcasted_iota(jnp.int32, (row.shape[0], size), 1) + k * size
        chosen.append((row[...] == ids).astype(F32).astype(BF16))
    acts = []
    for i in range(3):
        act = 0.0
        for k in range(n_moved):
            act = act + dot(chosen[k], moved[k][:, i * tokens : (i + 1) * tokens])
        if i < 2:
            act = act * scale[...]
        acts.append(dot(act.astype(BF16), order).astype(BF16))
    outs = (gate_o, up_o, down_o)
    slots = buf.shape[0]
    copies = []
    step = 0
    for m in range(n_mp):
        cols = cols_of(mp ^ m, width)
        for i in range(3):
            slot = step % slots
            if step >= slots:
                copies[step - slots].wait()
            for c in range(0, width, 256):
                e = min(c + 256, width)
                if i < 2:
                    block = toks[m][:, c:e]
                else:
                    lo, hi = m % 2, m // 2
                    block = jnp.concatenate(
                        [cots[2 * lo][hi, :, c:e], cots[2 * lo + 1][hi, :, c:e]], axis=0
                    )
                buf[slot, :, c:e] = dot(acts[i], block).astype(BF16)
            copy = pltpu.make_async_copy(
                buf.at[slot], outs[i].at[:, cols], sem.at[slot]
            )
            copy.start()
            copies.append(copy)
            step += 1
    for copy in copies[-slots:]:
        copy.wait()


VM = pl.BlockSpec(memory_space=pltpu.VMEM)
ANY = pl.BlockSpec(memory_space=pl.ANY)


def call(kernel, n_in, outs, out_specs, flops, nbytes, scratch=()):
    return pl.pallas_call(
        kernel,
        out_shape=outs,
        in_specs=[VM] * n_in,
        out_specs=out_specs,
        scratch_shapes=scratch,
        compiler_params=pltpu.CompilerParams(vmem_limit_bytes=LIMIT),
        cost_estimate=pl.CostEstimate(
            flops=flops, bytes_accessed=nbytes, transcendentals=0
        ),
    )


def device_pass(tokens, grad_out, gate_src, up_src, down_src, unit_map, copy_flag):
    n_dp = lax.axis_size("dp")
    n_mp = lax.axis_size("mp")
    rows, width = tokens.shape
    src_dev = gate_src.shape[0]
    wide_dev = unit_map.shape[0]
    quant = (wide_dev + 3 * n_dp - 1) // (3 * n_dp)
    slots = -(-3 * quant // 16) * 16
    n_tok = rows * n_dp
    half = n_dp // 2
    stages = outer_stages(n_dp)

    digits, top = 1, 256
    while top < 2 * src_dev * n_dp * n_mp:
        digits, top = digits + 1, top * 256
    lanes = -(-(digits * -(-wide_dev // 128)) // rows) * 128

    load = pl.pallas_call(
        functools.partial(pack_kernel, digits),
        out_shape=jax.ShapeDtypeStruct((rows, 2 * width + lanes), BF16),
        in_specs=[ANY] * 4,
        out_specs=VM,
        scratch_shapes=[
            pltpu.VMEM((1, wide_dev), jnp.int32),
            pltpu.VMEM((1, wide_dev), jnp.int32),
            pltpu.VMEM((rows, width), BF16),
            pltpu.VMEM((rows, width), BF16),
            pltpu.SemaphoreType.DMA((4,)),
        ],
        compiler_params=pltpu.CompilerParams(vmem_limit_bytes=60 * 1024 * 1024),
    )(tokens, grad_out, unit_map.reshape(1, -1), copy_flag.reshape(1, -1))
    for stride, radix in stages:
        load = jnp.concatenate(
            [load] + [swap(load, "dp", r * stride) for r in range(1, radix)], axis=0
        )
    t_own = load[:, : width + lanes]
    c_own = load[:, width + lanes :]
    t_far = swap(t_own, "dp", 1)
    c_hi = jnp.stack([c_own] + [swap(c_own, "mp", 2 * r) for r in range(1, n_mp // 2)])
    t_all = jnp.concatenate([t_own[:, :width], t_far[:, :width]], axis=0)
    t_hi = [t_all] + [swap(t_all, "mp", 2 * r) for r in range(1, n_mp // 2)]
    c_far = swap(c_hi, "dp", 1)
    toks = []
    for t in t_hi:
        toks += [t, swap(t, "mp", 1)]
    cots = [c_hi, c_far, swap(c_hi, "mp", 1), swap(c_far, "mp", 1)]

    pick, row, scale = call(
        functools.partial(table_kernel, digits, n_mp, rows, wide_dev, src_dev, slots),
        2,
        (
            jax.ShapeDtypeStruct((n_dp * slots, 1), jnp.int32),
            jax.ShapeDtypeStruct((wide_dev, 1), jnp.int32),
            jax.ShapeDtypeStruct((wide_dev, 1), F32),
        ),
        (VM,) * 3,
        0,
        n_dp * wide_dev * 512,
    )(t_own[:, width:], t_far[:, width:])

    act = jax.ShapeDtypeStruct((n_tok, src_dev), BF16)
    send_o = jax.ShapeDtypeStruct((n_dp * slots, 3 * n_tok), BF16)
    wbytes = src_dev * width * n_mp * 2
    mm = 2 * n_tok * src_dev * width * n_mp
    pre_t = jax.ShapeDtypeStruct((n_tok, src_dev), F32)
    half_t = jax.ShapeDtypeStruct((n_tok // 2, src_dev), F32)
    near = call(
        functools.partial(near_kernel, n_mp),
        7,
        (pre_t, pre_t, half_t),
        (VM,) * 3,
        3 * mm // 2,
        3 * wbytes,
    )(toks[0], toks[1], cots[0], cots[2], gate_src, up_src, down_src)
    hid, gpg, gpu, send = call(
        functools.partial(forward_kernel, n_dp, n_mp, rows),
        n_mp + 7,
        (act, act, act, send_o),
        (VM,) * 4,
        3 * mm // 2,
        3 * wbytes,
    )(*toks[2:], cots[1], cots[3], *near, gate_src, up_src, down_src, pick)
    moved = send.reshape(half, 2, slots, 3 * n_tok)
    inner = 1
    for stride, radix in stages:
        view = moved.reshape((half // (inner * radix), radix, inner) + moved.shape[1:])
        pieces = [view[:, 0]]
        pieces += [swap(view[:, r], "dp", r * stride) for r in range(1, radix)]
        inner *= radix
        moved = jnp.stack(pieces, axis=1).reshape(moved.shape)
    moved_far = swap(moved[:, 1], "dp", 1)
    moved = [p.reshape(-1, 3 * n_tok) for p in (moved[:, 0], moved_far)]

    keep_t = jax.ShapeDtypeStruct((n_mp // 2, n_tok, width), F32)
    send_t = jax.ShapeDtypeStruct((n_mp // 2, n_tok, width), BF16)

    def partial(acts, weights):
        k = len(acts)
        return call(
            functools.partial(partial_kernel, n_mp, k),
            2 * k,
            (keep_t, send_t),
            (VM, VM),
            k * mm,
            k * wbytes,
        )(*acts, *weights)

    in_keep, in_send = partial((gpg, gpu), (gate_src, up_src))
    out_keep, out_send = partial((hid,), (down_src,))

    def scatter(total, axis, stride, radix):
        parts = total.reshape((radix, -1) + total.shape[1:])
        out = parts[0]
        got = [swap(parts[r].astype(BF16), axis, r * stride) for r in range(1, radix)]
        for g in got:
            out = out + g.astype(F32)
        return out

    out_sum = out_keep + swap(out_send, "mp", 1).astype(F32)
    in_sum = in_keep + swap(in_send, "mp", 1).astype(F32)
    out_sum = scatter(out_sum, "mp", 2, n_mp // 2)[0]
    out_sum = scatter(out_sum, "dp", 1, 2)
    in_far = swap(in_sum[:, n_tok // 2 :].astype(BF16), "dp", 1)
    in_sum = in_sum[:, : n_tok // 2] + in_far.astype(F32)
    in_sum = scatter(in_sum, "mp", 2, n_mp // 2)[0]
    both = jnp.concatenate([out_sum, in_sum], axis=1)
    for stride, radix in reversed(stages):
        both = scatter(both, "dp", stride, radix)

    wide_t = jax.ShapeDtypeStruct((wide_dev, n_mp * width), BF16)
    grad_gate, grad_up, grad_down = call(
        functools.partial(widen_kernel, n_dp, n_mp, rows, len(moved)),
        n_mp + 6 + len(moved),
        (wide_t,) * 3,
        (ANY,) * 3,
        6 * n_tok * wide_dev * width * n_mp,
        3 * wide_dev * width * n_mp * 2,
        (pltpu.VMEM((4, wide_dev, width), BF16), pltpu.SemaphoreType.DMA((4,))),
    )(*toks, *cots, *moved, row, scale)
    return (
        both[:, :width].astype(BF16),
        both[:, width:].astype(BF16),
        grad_gate,
        grad_up,
        grad_down,
    )


def solution(mesh):
    rows = P(("dp", "mp"), None)
    tile = P("dp", "mp")
    unit = P(("dp", "mp"))
    return jax.shard_map(
        device_pass,
        mesh=mesh,
        in_specs=(tile, tile, rows, rows, rows, unit, unit),
        out_specs=(tile, tile, rows, rows, rows),
        check_vma=False,
    )
```

```python
import functools

import jax
import jax.numpy as jnp
from jax import lax
from jax.experimental import pallas as pl
from jax.experimental.pallas import tpu as pltpu
from jax.sharding import PartitionSpec as P


F32 = jnp.float32
BF16 = jnp.bfloat16
LIMIT = 12 * 1024 * 1024
NT = (((1,), (1,)), ((), ()))
NN = (((1,), (0,)), ((), ()))


def dot(a, b, dims=NN):
    return lax.dot_general(a, b, dims, preferred_element_type=F32)


def swap(x, axis, offset):
    n = lax.axis_size(axis)
    return lax.ppermute(x, axis, [(i, i ^ offset) for i in range(n)])


def outer_stages(n):
    stages, stride = [], 2
    while stride < n:
        radix = 4 if stride * 4 <= n else 2
        stages.append((stride, radix))
        stride *= radix
    return stages


def token_order(dp, n_dp, rows):
    half = n_dp // 2
    tokens = n_dp * rows
    place = lax.broadcasted_iota(jnp.int32, (tokens, tokens), 0)
    held = lax.broadcasted_iota(jnp.int32, (tokens, tokens), 1)
    block = held // rows
    offset = block // half + 2 * (block % half)
    return (place == (dp ^ offset) * rows + held % rows).astype(F32).astype(BF16)


def cols_of(index, width):
    return pl.ds(pl.multiple_of(index * width, 128), width)


def pack_kernel(digits, tok, cot, umap_i, flag_i, out, umap, flag, sem):
    rows, width = tok.shape
    wide = umap.shape[1]
    lanes = out.shape[1] - 2 * width
    moves = (
        (umap_i, umap),
        (flag_i, flag),
        (tok, out.at[:, :width]),
        (cot, out.at[:, width + lanes :]),
    )
    copies = []
    for i, (src, dst) in enumerate(moves):
        copies.append(pltpu.make_async_copy(src, dst, sem.at[i]))
        copies[-1].start()
    copies[0].wait()
    copies[1].wait()
    code = umap[...] * 2 + flag[...]
    chunks = -(-wide // 128)
    code = jnp.concatenate(
        [code, jnp.zeros((1, chunks * 128 - wide), jnp.int32)], axis=1
    ) if chunks * 128 > wide else code
    parts = []
    for d in range(digits):
        digit = ((code >> (8 * d)) & 255).astype(F32)
        parts += [digit[:, 128 * c : 128 * c + 128] for c in range(chunks)]
    zero = jnp.zeros((1, 128), F32)
    parts += [zero] * (rows * lanes // 128 - len(parts))
    for b in range(lanes // 128):
        block = jnp.concatenate(parts[b * rows : (b + 1) * rows], axis=0)
        out[:, width + 128 * b : width + 128 * b + 128] = block.astype(BF16)
    copies[2].wait()
    copies[3].wait()


def table_kernel(digits, n_mp, rows, wide, src_dev, slots, near, far, pick_o, row_o, scale_o):
    mp = lax.axis_index("mp")
    dp = lax.axis_index("dp")
    half = near.shape[0] // rows
    chunks = -(-wide // 128)
    span = chunks * 128
    held = (near[...].astype(F32), far[...].astype(F32))

    def code_of(offset):
        part = held[offset % 2]
        first = (offset // 2) * rows
        pieces = []
        for c in range(chunks):
            total = 0.0
            for d in range(digits):
                k = d * chunks + c
                r, b = first + k % rows, k // rows
                total = total + part[r : r + 1, 128 * b : 128 * b + 128] * float(256**d)
            pieces.append(total)
        return jnp.concatenate(pieces, axis=1)

    n_dp = 2 * half
    code = jnp.concatenate([code_of(o) for o in range(n_dp)], axis=0).astype(jnp.int32)
    flags = (code & 1).astype(F32)
    maps = (code >> 1).astype(F32)
    lane = lax.broadcasted_iota(jnp.int32, (1, span), 1)
    valid = lane < wide
    lane_w = lax.broadcasted_iota(jnp.int32, (wide, span), 1)
    unit_w = lax.broadcasted_iota(jnp.int32, (wide, span), 0)
    eye = lane_w == unit_w

    def column(row):
        return jnp.sum(jnp.where(eye, row, 0.0), axis=1, keepdims=True)

    map_col = column(maps[0:1])
    flag_col = column(flags[0:1])
    share = jnp.zeros((wide, span), F32)
    for o in range(n_dp):
        share = share + jnp.where(maps[o : o + 1] == map_col, flags[o : o + 1], 0.0)
    share = jnp.sum(share, axis=1, keepdims=True)
    scale_o[...] = flag_col / share

    def owner_of(m):
        return jnp.floor((m + 0.5) * (1.0 / (src_dev * n_mp)))

    owner = jnp.where(valid, owner_of(maps[0:1]), -1.0)
    owner_col = owner_of(map_col)
    earlier = (owner == owner_col) & (lane_w < unit_w)
    arrival = jnp.sum(jnp.where(earlier, 1.0, 0.0), axis=1, keepdims=True)
    offset = owner_col.astype(jnp.int32) ^ dp
    place = (offset & 1) * half + (offset >> 1)
    row_o[...] = place * slots + arrival.astype(jnp.int32)

    local = maps - ((dp * n_mp + mp) * src_dev).astype(F32)
    owned = (local >= 0.0) & (local < float(src_dev)) & valid
    mine = jnp.where(owned, 1.0, 0.0)
    low = lax.broadcasted_iota(jnp.int32, (span, span), 0)
    high = lax.broadcasted_iota(jnp.int32, (span, span), 1)
    before = jnp.where(low < high, 1.0, 0.0).astype(BF16)
    rank = dot(mine.astype(BF16), before)
    rank = jnp.where(owned, rank, -1.0).astype(jnp.int32)
    slot = lax.broadcasted_iota(jnp.int32, (slots, span), 0)
    for o in range(n_dp):
        hit = jnp.where(rank[o : o + 1] == slot, local[o : o + 1] + 1.0, 0.0)
        chosen = jnp.sum(hit, axis=1, keepdims=True) - 1.0
        pick_o[o * slots : (o + 1) * slots, :] = chosen.astype(jnp.int32)


def load_kernel(*refs):
    copies = []
    for i in range(3):
        copies.append(pltpu.make_async_copy(refs[i], refs[3 + i], refs[6].at[i]))
        copies[-1].start()
    for copy in copies:
        copy.wait()


def both_rows(near, far, width):
    return jnp.concatenate([near[:, :width], far[:, :width]], axis=0)


def near_kernel(n_mp, t0, t1, f0, f1, gate, up, gate_o, up_o):
    mp = lax.axis_index("mp")
    width = gate.shape[1] // n_mp
    pre_gate = pre_up = 0.0
    for m, (near, far) in enumerate(((t0, f0), (t1, f1))):
        cols = cols_of(mp ^ m, width)
        t = both_rows(near, far, width)
        pre_gate = pre_gate + dot(t, gate[:, cols], NT)
        pre_up = pre_up + dot(t, up[:, cols], NT)
    gate_o[...] = pre_gate
    up_o[...] = pre_up


def middle_kernel(n_mp, *refs):
    toks, refs = refs[: n_mp - 2], refs[n_mp - 2 :]
    cots, refs = refs[:n_mp], refs[n_mp:]
    cots_far, refs = refs[:2], refs[2:]
    gate, up, down, gate_o, up_o, grad_o, far_o = refs
    mp = lax.axis_index("mp")
    width = gate.shape[1] // n_mp
    pre_gate = pre_up = grad_near = grad_far = 0.0
    for m in range(2, n_mp):
        cols = cols_of(mp ^ m, width)
        t = toks[m - 2][:, :width]
        pre_gate = pre_gate + dot(t, gate[:, cols], NT)
        pre_up = pre_up + dot(t, up[:, cols], NT)
    for m in range(2):
        c = jnp.concatenate([cots[m][...], cots_far[m][...]], axis=0)
        g = dot(c, down[:, cols_of(mp ^ m, width)], NT)
        grad_near = grad_near + g[: g.shape[0] // 2]
        grad_far = grad_far + g[g.shape[0] // 2 :]
    for m in range(2, n_mp):
        grad_near = grad_near + dot(cots[m][...], down[:, cols_of(mp ^ m, width)], NT)
    gate_o[...] = pre_gate
    up_o[...] = pre_up
    grad_o[...] = grad_near
    far_o[...] = grad_far


def forward_kernel(n_mp, *refs):
    toks, refs = refs[: n_mp - 2], refs[n_mp - 2 :]
    cots, refs = refs[: n_mp - 2], refs[n_mp - 2 :]
    gate_i, up_i, gate_n, up_n, grad_n, grad_f, refs = *refs[:6], refs[6:]
    gate, up, down, hid_o, gpg_o, gpu_o = refs
    mp = lax.axis_index("mp")
    width = gate.shape[1] // n_mp
    pre_gate = pre_up = 0.0
    grad_far = grad_f[...]
    for m in range(2, n_mp):
        cols = cols_of(mp ^ m, width)
        t = toks[m - 2][:, :width]
        pre_gate = pre_gate + dot(t, gate[:, cols], NT)
        pre_up = pre_up + dot(t, up[:, cols], NT)
        grad_far = grad_far + dot(cots[m - 2][...], down[:, cols], NT)
    pre_gate = gate_i[...] + jnp.concatenate([gate_n[...], pre_gate], axis=0)
    pre_up = up_i[...] + jnp.concatenate([up_n[...], pre_up], axis=0)
    grad_hidden = jnp.concatenate([grad_n[...], grad_far], axis=0)
    sigma = jax.nn.sigmoid(pre_gate)
    active = pre_gate * sigma
    hid_o[...] = (active * pre_up).astype(BF16)
    slope = sigma + active * (1.0 - sigma)
    gpg_o[...] = (grad_hidden * pre_up * slope).astype(BF16)
    gpu_o[...] = (grad_hidden * active).astype(BF16)


def choose_kernel(n_dp, rows, gpg, gpu, hid, pick, send_o):
    dp = lax.axis_index("dp")
    order = token_order(dp, n_dp, rows)
    chosen = pick[...] == lax.broadcasted_iota(
        jnp.int32, (pick.shape[0], gpg.shape[1]), 1
    )
    chosen = chosen.astype(F32).astype(BF16)
    acts = [dot(order, act[...]).astype(BF16) for act in (gpg, gpu, hid)]
    sent = dot(chosen, jnp.concatenate(acts, axis=0), NT).astype(BF16)
    send_o[...] = sent


def in_sum_kernel(keep, got, first_o, second_o, high_o, low_o):
    cut = low_o.shape[0]
    total = keep[...] + got[...].astype(F32)
    first_o[...] = total[1:, cut:].astype(BF16)
    second_o[...] = total[0, cut:].astype(BF16)
    high_o[...] = total[1:, :cut]
    low_o[...] = total[0, :cut]


def out_sum_kernel(keep, got, first_o, second_o, far_o, near_o):
    cut = near_o.shape[0]
    total = keep[...] + got[...].astype(F32)
    first_o[...] = total[1:, cut:].astype(BF16)
    second_o[...] = total[1:, :cut].astype(BF16)
    far_o[...] = total[0, cut:]
    near_o[...] = total[0, :cut]


def add_kernel(keep, *refs):
    total = keep[...]
    for got in refs[:-1]:
        total = total + got[...].astype(F32)
    refs[-1][...] = total.astype(BF16)


def partial_kernel(n_mp, n_terms, first, *refs):
    acts, refs = refs[:n_terms], refs[n_terms:]
    weights, out = refs[:n_terms], refs[n_terms]
    mp = lax.axis_index("mp")
    width = out.shape[2]
    for m in range(first, n_mp, 2):
        cols = cols_of(mp ^ m, width)
        total = dot(acts[0][...], weights[0][:, cols])
        for a, w in zip(acts[1:], weights[1:]):
            total = total + dot(a[...], w[:, cols])
        out[m // 2] = total.astype(out.dtype)


def widen_kernel(n_dp, n_mp, rows, n_moved, *refs):
    rights = []
    for _ in range(2):
        rights.append(list(zip(refs[:n_mp], refs[n_mp : 2 * n_mp])))
        refs = refs[2 * n_mp :]
    toks, cots = rights
    moved, refs = refs[:n_moved], refs[n_moved:]
    row, scale, gate_o, up_o, down_o, buf, sem = refs
    mp = lax.axis_index("mp")
    dp = lax.axis_index("dp")
    tokens = n_dp * rows
    width = buf.shape[2]
    order = token_order(dp, n_dp, rows)
    arrived = jnp.concatenate([m[...] for m in moved], axis=0)
    ids = lax.broadcasted_iota(jnp.int32, (row.shape[0], arrived.shape[0]), 1)
    chosen = (row[...] == ids).astype(F32).astype(BF16)
    taken = dot(chosen, arrived)
    acts = []
    for i in range(3):
        act = taken[:, i * tokens : (i + 1) * tokens]
        if i < 2:
            act = act * scale[...]
        acts.append(dot(act.astype(BF16), order).astype(BF16))
    outs = (gate_o, up_o, down_o)
    slots = buf.shape[0]
    copies = []
    step = 0
    for m in range(n_mp):
        cols = cols_of(mp ^ m, width)
        for i in range(3):
            slot = step % slots
            if step >= slots:
                copies[step - slots].wait()
            near, far = (toks if i < 2 else cots)[m]
            for c in range(0, width, 256):
                e = min(c + 256, width)
                block = jnp.concatenate([near[:, c:e], far[:, c:e]], axis=0)
                buf[slot, :, c:e] = dot(acts[i], block).astype(BF16)
            copy = pltpu.make_async_copy(
                buf.at[slot], outs[i].at[:, cols], sem.at[slot]
            )
            copy.start()
            copies.append(copy)
            step += 1
    for copy in copies[-slots:]:
        copy.wait()


VM = pl.BlockSpec(memory_space=pltpu.VMEM)
ANY = pl.BlockSpec(memory_space=pl.ANY)


def call(kernel, n_in, outs, out_specs, flops, nbytes, scratch=()):
    return pl.pallas_call(
        kernel,
        out_shape=outs,
        in_specs=[VM] * n_in,
        out_specs=out_specs,
        scratch_shapes=scratch,
        compiler_params=pltpu.CompilerParams(vmem_limit_bytes=LIMIT),
        cost_estimate=pl.CostEstimate(
            flops=flops, bytes_accessed=nbytes, transcendentals=0
        ),
    )


def device_pass(tokens, grad_out, gate_src, up_src, down_src, unit_map, copy_flag):
    n_dp = lax.axis_size("dp")
    n_mp = lax.axis_size("mp")
    rows, width = tokens.shape
    src_dev = gate_src.shape[0]
    wide_dev = unit_map.shape[0]
    quant = (wide_dev + 3 * n_dp - 1) // (3 * n_dp)
    slots = -(-3 * quant // 16) * 16
    n_tok = rows * n_dp
    half = n_dp // 2
    stages = outer_stages(n_dp)

    digits, top = 1, 256
    while top < 2 * src_dev * n_dp * n_mp:
        digits, top = digits + 1, top * 256
    lanes = -(-(digits * -(-wide_dev // 128)) // rows) * 128

    load = pl.pallas_call(
        functools.partial(pack_kernel, digits),
        out_shape=jax.ShapeDtypeStruct((rows, 2 * width + lanes), BF16),
        in_specs=[ANY] * 4,
        out_specs=VM,
        scratch_shapes=[
            pltpu.VMEM((1, wide_dev), jnp.int32),
            pltpu.VMEM((1, wide_dev), jnp.int32),
            pltpu.SemaphoreType.DMA((4,)),
        ],
        compiler_params=pltpu.CompilerParams(vmem_limit_bytes=60 * 1024 * 1024),
    )(tokens, grad_out, unit_map.reshape(1, -1), copy_flag.reshape(1, -1))
    for stride, radix in stages:
        got = [swap(load, "dp", r * stride) for r in range(1, radix)]
        load = jnp.concatenate([load] + got, axis=0)

    def cores(blocks):
        return [b for x in blocks for b in (x, swap(x, "mp", 1))]

    highs = range(1, n_mp // 2)
    t_own, c_own = load[:, : width + lanes], load[:, width + lanes :]
    t_far = swap(t_own, "dp", 1)
    t_rows = cores([t_own] + [swap(t_own, "mp", 2 * r) for r in highs])
    t_rows_far = cores([t_far] + [swap(t_far, "mp", 2 * r) for r in highs])
    c_hi = [c_own] + [swap(c_own, "mp", 2 * r) for r in highs]
    c_far = [swap(c, "dp", 1) for c in c_hi]
    c_rows = cores(c_hi)
    c_rows_far = cores(c_far)

    gate_src, up_src, down_src = pl.pallas_call(
        load_kernel,
        out_shape=[jax.ShapeDtypeStruct(w.shape, BF16) for w in (gate_src,) * 3],
        in_specs=[ANY] * 3,
        out_specs=[VM] * 3,
        scratch_shapes=[pltpu.SemaphoreType.DMA((3,))],
        compiler_params=pltpu.CompilerParams(vmem_limit_bytes=40 * 1024 * 1024),
        cost_estimate=pl.CostEstimate(
            flops=0, bytes_accessed=6 * src_dev * width * n_mp, transcendentals=0
        ),
    )(gate_src, up_src, down_src)

    pick, row, scale = call(
        functools.partial(table_kernel, digits, n_mp, rows, wide_dev, src_dev, slots),
        2,
        (
            jax.ShapeDtypeStruct((n_dp * slots, 1), jnp.int32),
            jax.ShapeDtypeStruct((wide_dev, 1), jnp.int32),
            jax.ShapeDtypeStruct((wide_dev, 1), F32),
        ),
        (VM,) * 3,
        0,
        n_dp * wide_dev * 512,
    )(t_own[:, width:], t_far[:, width:])

    act = jax.ShapeDtypeStruct((n_tok, src_dev), BF16)
    send_o = jax.ShapeDtypeStruct((n_dp * slots, 3 * n_tok), BF16)
    wbytes = src_dev * width * n_mp * 2
    mm = 2 * n_tok * src_dev * width * n_mp
    pre_t = jax.ShapeDtypeStruct((n_tok, src_dev), F32)
    half_t = jax.ShapeDtypeStruct((n_tok // 2, src_dev), F32)
    near = call(
        functools.partial(near_kernel, n_mp), 6, (pre_t, pre_t), (VM,) * 2, mm, wbytes
    )(*t_rows[:2], *t_rows_far[:2], gate_src, up_src)
    middle = call(
        functools.partial(middle_kernel, n_mp),
        2 * n_mp + 3,
        (half_t,) * 4,
        (VM,) * 4,
        3 * mm // 2,
        2 * wbytes,
    )(*t_rows[2:], *c_rows, *c_rows_far[:2], gate_src, up_src, down_src)
    hid, gpg, gpu = call(
        functools.partial(forward_kernel, n_mp),
        2 * n_mp + 5,
        (act,) * 3,
        (VM,) * 3,
        mm // 2,
        wbytes,
    )(*t_rows_far[2:], *c_rows_far[2:], *near, *middle, gate_src, up_src, down_src)
    send = call(
        functools.partial(choose_kernel, n_dp, rows),
        4,
        send_o,
        VM,
        6 * n_dp * slots * src_dev * n_tok,
        4 * n_tok * src_dev,
    )(gpg, gpu, hid, pick)
    moved = send.reshape(half, 2, slots, 3 * n_tok)
    inner = 1
    for stride, radix in stages:
        view = moved.reshape((half // (inner * radix), radix, inner) + moved.shape[1:])
        pieces = [view[:, 0]]
        pieces += [swap(view[:, r], "dp", r * stride) for r in range(1, radix)]
        inner *= radix
        moved = jnp.stack(pieces, axis=1).reshape(moved.shape)
    moved_far = swap(moved[:, 1], "dp", 1)
    moved = [p.reshape(-1, 3 * n_tok) for p in (moved[:, 0], moved_far)]

    keep_t = jax.ShapeDtypeStruct((n_mp // 2, n_tok, width), F32)
    send_t = jax.ShapeDtypeStruct((n_mp // 2, n_tok, width), BF16)

    def partial(first, out, acts, weights):
        k = len(acts)
        return call(
            functools.partial(partial_kernel, n_mp, k, first),
            2 * k,
            out,
            VM,
            k * mm // 2,
            k * wbytes // 2,
        )(*acts, *weights)

    in_args = ((gpg, gpu), (gate_src, up_src))
    out_args = ((hid,), (down_src,))
    in_send = partial(1, send_t, *in_args)
    out_send = partial(1, send_t, *out_args)
    in_keep = partial(0, keep_t, *in_args)
    out_keep = partial(0, keep_t, *out_args)

    def added(x, got):
        for g in got:
            x = x + g.astype(F32)
        return x

    hi, cut = n_mp // 2, n_tok // 2
    one, many = (cut, width), (hi - 1, cut, width)

    def summed(kernel, args, *outs):
        return call(
            kernel, len(args), outs, (VM,) * len(outs), args[0].size, 8 * args[0].size
        )(*args)

    def typed(shape, kind):
        return jax.ShapeDtypeStruct(shape, kind)

    def swap_high(x):
        return [swap(x[r - 1], "mp", 2 * r) for r in highs]

    in_first, in_second, in_high, in_low = summed(
        in_sum_kernel, (in_keep, swap(in_send, "mp", 1)),
        typed(many, BF16), typed(one, BF16), typed(many, F32), typed(one, F32),
    )
    out_first, out_second, out_far, out_near = summed(
        out_sum_kernel, (out_keep, swap(out_send, "mp", 1)),
        typed(many, BF16), typed(many, BF16), typed(one, F32), typed(one, F32),
    )
    in_first = swap(in_first, "dp", 1)
    in_second = swap(in_second, "dp", 1)
    out_first = swap_high(out_first)
    out_second = swap_high(out_second)
    (in_send,) = summed(add_kernel, (in_high, in_first), typed(many, BF16))
    (out_send,) = summed(add_kernel, (out_far, *out_first), typed(one, BF16))
    in_sum = added(in_low, [in_second] + swap_high(in_send))
    out_sum = added(out_near, out_second + [swap(out_send, "dp", 1)])
    both = jnp.concatenate([out_sum, in_sum], axis=1)
    for stride, radix in reversed(stages):
        parts = both.reshape((radix, -1) + both.shape[1:])
        both = added(
            parts[0],
            [swap(parts[r].astype(BF16), "dp", r * stride) for r in range(1, radix)],
        )
    layer_out = both[:, :width].astype(BF16)
    grad_tokens = both[:, width:].astype(BF16)

    wide_t = jax.ShapeDtypeStruct((wide_dev, n_mp * width), BF16)
    grad_gate, grad_up, grad_down = call(
        functools.partial(widen_kernel, n_dp, n_mp, rows, len(moved)),
        4 * n_mp + 2 + len(moved),
        (wide_t,) * 3,
        (ANY,) * 3,
        6 * n_tok * wide_dev * width * n_mp,
        3 * wide_dev * width * n_mp * 2,
        (pltpu.VMEM((4, wide_dev, width), BF16), pltpu.SemaphoreType.DMA((4,))),
    )(*t_rows, *t_rows_far, *c_rows, *c_rows_far, *moved, row, scale)
    return (
        layer_out,
        grad_tokens,
        grad_gate,
        grad_up,
        grad_down,
    )


def solution(mesh):
    rows = P(("dp", "mp"), None)
    tile = P("dp", "mp")
    unit = P(("dp", "mp"))
    return jax.shard_map(
        device_pass,
        mesh=mesh,
        in_specs=(tile, tile, rows, rows, rows, unit, unit),
        out_specs=(tile, tile, rows, rows, rows),
        check_vma=False,
    )
```
